256 devices in a mesh: dp: 32 (over x, z), tensor: 8 (over y, core).
Axes of the slice: x: 4, y: 4, z: 8, core: 2. Of those that a mesh axis runs over, the one named last changes fastest.
Arguments:
- tubelets: bfloat16 [1024, 32, 4096], P('dp', 'tensor'), may hold values from -6 to 6
- keep_index: int32 [1024, 32], P('dp', 'tensor'), may hold values from -1 to 31, as said below
- dest_row: int32 [1024, 32], P('dp', 'tensor'), may hold values from -1 to 31, as said below
- dest_slot: int32 [1024, 32], P('dp', 'tensor'), may hold values from -1 to 1023, as said below
- segment: int32 [32, 1024], P('dp'), may hold values from -1 to 1023, as said below
- ln_gain: bfloat16 [4096], replicated, may hold values from 0.25 to 1.75
- w_query: bfloat16 [4096, 3072], P('dp', 'tensor')
- w_key: bfloat16 [4096, 3072], P('dp', 'tensor')
- w_value: bfloat16 [4096, 3072], P('dp', 'tensor'), may hold values from -0.09375 to 0.09375
Outputs:
- attended: bfloat16 [32, 1024, 3072], P('dp', None, 'tensor')
The draws below stay inside these ranges and needn't reach their ends.
Inputs may be any that keep to these rules, and one draw needn't show every extreme that they name: `keep_index`: entry e of a clip's list belongs to tensor index e // 4 and, when kept, names a tubelet of that index's share, each at most once; -1 marks a dropped entry. Each share keeps 1 to 4 tubelets. `dest_row`: -1 exactly where keep_index is -1. A clip goes whole to one row; each row receives exactly one clip from each dp index, so at most 4 kept tubelets go from one device to one row; some dp index sends that many to every row. `dest_slot`: -1 exactly where keep_index is -1. A kept tubelet on tensor index j lands in slots j * 128 to (j + 1) * 128 - 1; no two kept tubelets share a row and a slot; some row has all its slots filled. `segment`: the clip whose tubelet fills each slot, clips numbered in the order of the tubelets array; -1 for an empty slot. Agrees with dest_row and dest_slot.
All inputs are finite; a program needn't handle non-finite values.
Results may differ from the reference program's by a relative error of at most 0.0082.
Values may be sent and summed in bfloat16 or wider, within the bound.
A program may use at most 64 MiB of HBM per device.

```python
import math
import jax
import jax.numpy as jnp
from jax import lax

D = 4096
HEADS = 24
HS = 128
NT_DEV = 4
CLIPS_DEV = 32
TOK_DEV = 128
ROWS = 32
ROW_LEN = 1024
CLIPS = 1024
CLIP_TUB = 32


def packing_plan(key):
    seeded = jax.random.fold_in(key, 4242)
    keys_list = jax.random.split(seeded, 6)
    tensor_count = CLIP_TUB // NT_DEV
    shifts = jax.random.permutation(keys_list[0], ROWS).astype(jnp.int32)
    clip_ids = jnp.arange(CLIPS, dtype=jnp.int32)
    sources = clip_ids // CLIPS_DEV
    locals_in = clip_ids % CLIPS_DEV
    row_of = (sources + shifts[locals_in % ROWS]) % ROWS
    lowest = jax.random.randint(keys_list[1], (ROWS,), 1, NT_DEV + 1).astype(jnp.int32)
    extra_kept = jax.random.randint(keys_list[2], (CLIPS, tensor_count), 0, 1 << 20).astype(jnp.int32)
    extra_kept = extra_kept % (NT_DEV + 1 - lowest[sources])[:, None]
    counts = lowest[sources][:, None] + extra_kept
    full_source = jax.random.randint(keys_list[3], (), 0, ROWS).astype(jnp.int32)
    full_row = jax.random.randint(keys_list[4], (), 0, ROWS).astype(jnp.int32)
    forced = (sources == full_source) | (row_of == full_row)
    counts = jnp.where(forced[:, None], NT_DEV, counts).astype(jnp.int32)
    scores = jax.random.randint(keys_list[5], (CLIPS, tensor_count, NT_DEV), 0, 1 << 20).astype(jnp.int32)
    scores = scores * NT_DEV + jnp.arange(NT_DEV, dtype=jnp.int32)
    within = jnp.argsort(scores, axis=-1, stable=True).astype(jnp.int32)
    positions = jnp.arange(NT_DEV, dtype=jnp.int32)
    is_kept = positions[None, None, :] < counts[:, :, None]
    share_ids = jnp.arange(tensor_count, dtype=jnp.int32)[None, :, None]
    keep_index = jnp.where(is_kept, share_ids * NT_DEV + within, -1).astype(jnp.int32)
    by_row = jnp.argsort(row_of, stable=True).astype(jnp.int32)
    sorted_counts = counts[by_row].reshape(ROWS, CLIPS_DEV, tensor_count)
    starts = (jnp.cumsum(sorted_counts, axis=1) - sorted_counts).reshape(CLIPS, tensor_count).astype(jnp.int32)
    offsets = jnp.zeros((CLIPS, tensor_count), jnp.int32).at[by_row].set(starts)
    slot_ids = jnp.where(is_kept, share_ids * TOK_DEV + offsets[:, :, None] + positions[None, None, :], -1).astype(jnp.int32)
    row_ids = jnp.where(is_kept, row_of[:, None, None], -1).astype(jnp.int32)
    flat_target = jnp.where(is_kept, row_of[:, None, None] * ROW_LEN + slot_ids, ROWS * ROW_LEN).reshape(-1)
    owners = jnp.broadcast_to(clip_ids[:, None, None], is_kept.shape).reshape(-1)
    segment = jnp.full((ROWS * ROW_LEN,), -1, jnp.int32).at[flat_target].set(owners, mode='drop')
    return (keep_index.reshape(CLIPS, CLIP_TUB), row_ids.reshape(CLIPS, CLIP_TUB), slot_ids.reshape(CLIPS, CLIP_TUB), segment.reshape(ROWS, ROW_LEN))


def draw_keep_index(key, part):
    return packing_plan(key)[0]


def draw_dest_row(key, part):
    return packing_plan(key)[1]


def draw_dest_slot(key, part):
    return packing_plan(key)[2]


def draw_segment(key, part):
    return packing_plan(key)[3]


def query_base(key):
    noise_draw = jax.random.normal(jax.random.fold_in(key, 811), (D, HEADS * HS), jnp.float32)
    return jnp.clip(noise_draw, -5.0, 5.0) / math.sqrt(D)


def draw_w_query(key, part):
    return query_base(key).astype(jnp.bfloat16)


def draw_w_key(key, part):
    fresh_noise = jax.random.normal(jax.random.fold_in(key, 812), (D, HEADS * HS), jnp.float32)
    fresh_noise = jnp.clip(fresh_noise, -5.0, 5.0) / math.sqrt(D)
    return fresh_noise.astype(jnp.bfloat16)


def steps_of(key, extent, cuts, least, top_value):
    loudness, own = 1.0, jax.random.fold_in(key, 6)
    for axis_at, parts in cuts:
        heights = jnp.exp(jax.random.uniform(jax.random.fold_in(own, axis_at), (parts,), jnp.float32, least / len(cuts), top_value / len(cuts)))
        loudness = loudness * jnp.repeat(heights, extent[axis_at] // parts).reshape([-1 if axis == axis_at else 1 for axis in range(len(extent))])
    return loudness


def gaussian(stream_key, dims, deviation, reach, cuts=(), kind=jnp.bfloat16):
    drawn = deviation * jax.random.normal(stream_key, dims, jnp.float32)
    if cuts:
        drawn = drawn * steps_of(stream_key, dims, cuts, -0.22, 0.18)
    return jnp.clip(drawn, -reach, reach).astype(kind)


def setup_inputs(seed: int = 0) -> dict:
    seeds = jax.random.split(jax.random.key(seed), 10)
    return {
        "tubelets": gaussian(seeds[0], (CLIPS, CLIP_TUB, D), 1.0, 6.0, ((0, 32), (1, 8))),
        "keep_index": draw_keep_index(jax.random.fold_in(seeds[9], 71), 0),
        "dest_row": draw_dest_row(jax.random.fold_in(seeds[9], 71), 0),
        "dest_slot": draw_dest_slot(jax.random.fold_in(seeds[9], 71), 0),
        "segment": draw_segment(jax.random.fold_in(seeds[9], 71), 0),
        "ln_gain": jnp.clip(1.0 + 0.15 * jax.random.normal(seeds[5], (D,), jnp.float32), 0.25, 1.75).astype(jnp.bfloat16),
        "w_query": draw_w_query(jax.random.fold_in(seeds[9], 71), 0),
        "w_key": draw_w_key(jax.random.fold_in(seeds[9], 71), 0),
        "w_value": gaussian(seeds[8], (D, HEADS * HS), D ** -0.5, 0.09375, ((0, 32), (1, 8))),
    }


block_rows = 512

def layer_norm(values_in, ln_gain):
    floats = values_in.astype(jnp.float32)
    average = lax.optimization_barrier(jnp.mean(floats, axis=-1, keepdims=True))
    centred = floats - average
    variance = lax.optimization_barrier(jnp.mean(centred * centred, axis=-1, keepdims=True))
    return (centred * lax.rsqrt(variance + 1e-06) * ln_gain.astype(jnp.float32)).astype(jnp.bfloat16)

def attend(query_rows, key_rows, value_rows, seg_query, seg_key):
    scores = jnp.einsum('qhd,khd->hqk', query_rows.astype(jnp.float32), key_rows.astype(jnp.float32))
    allowed = (seg_query[:, None] == seg_key[None, :]) & (seg_key[None, :] >= 0)
    masked = jnp.where(allowed[None], scores, -1e+30)
    largest = lax.optimization_barrier(jnp.max(masked, axis=-1, keepdims=True))
    weights = jnp.where(allowed[None], jnp.exp(masked - largest), 0.0)
    totals = lax.optimization_barrier(jnp.sum(weights, axis=-1, keepdims=True))
    totals = jnp.where(totals > 0, totals, 1.0)
    weights_bf = (weights / totals).astype(jnp.bfloat16)
    mixed = jnp.einsum('hqk,khd->qhd', weights_bf.astype(jnp.float32), value_rows.astype(jnp.float32))
    return mixed.astype(jnp.bfloat16)

def reference(tubelets, keep_index, dest_row, dest_slot, segment, ln_gain, w_query, w_key, w_value):
    is_kept = keep_index >= 0
    kept_rows = jnp.take_along_axis(tubelets, jnp.maximum(keep_index, 0).astype(jnp.int32)[:, :, None], axis=1)
    targets = jnp.where(is_kept, dest_row * ROW_LEN + dest_slot, ROWS * ROW_LEN).astype(jnp.int32)
    packed = jnp.zeros((ROWS * ROW_LEN + 1, D), jnp.bfloat16)
    packed = packed.at[targets.reshape(-1)].set(kept_rows.reshape(-1, D))
    packed = packed[:-1].reshape(ROWS, ROW_LEN, D)

    def one_row(row_item):
        packed_row, seg_row = row_item
        normed = layer_norm(packed_row, ln_gain)
        query_rows = (jnp.dot(normed, w_query, preferred_element_type=jnp.float32) * HS ** (-0.5)).astype(jnp.bfloat16)
        key_rows = jnp.dot(normed, w_key, preferred_element_type=jnp.float32).astype(jnp.bfloat16)
        value_rows = jnp.dot(normed, w_value, preferred_element_type=jnp.float32).astype(jnp.bfloat16)
        query_rows = query_rows.reshape(ROW_LEN // block_rows, block_rows, HEADS, HS)
        key_rows = key_rows.reshape(ROW_LEN, HEADS, HS)
        value_rows = value_rows.reshape(ROW_LEN, HEADS, HS)
        seg_blocks = seg_row.reshape(ROW_LEN // block_rows, block_rows)
        mixed = lax.map(lambda pair_in: attend(pair_in[0], key_rows, value_rows, pair_in[1], seg_row), (query_rows, seg_blocks))
        return mixed.reshape(ROW_LEN, HEADS * HS)
    return lax.map(one_row, (packed, segment))
```

```python
import jax
import jax.numpy as jnp
from jax import lax
from jax.experimental import pallas as pl
from jax.experimental.pallas import tpu as pltpu
from jax.sharding import PartitionSpec as P

MESH = pl.DeviceIdType.MESH
F32 = jnp.float32
BF16 = jnp.bfloat16
HS = 128
NX, NZ, NY = 4, 8, 4
NDP, NT = NX * NZ, 2 * NY
KEEP = 4
HEADS = 3
BLK = 128

A_ROWS, A_PLUS = 48, 16
B_ROWS = BLK - A_ROWS
BZ_PLUS, BX_PLUS = 32, 32

W_KEYS = (
    [("ax", d, t) for t in (1, 2) for d in (0, 1)]
    + [("bz", d, t) for t in (1, 2, 3, 4) for d in (0, 1)]
    + [("az", d, t) for t in (1, 2, 3, 4) for d in (0, 1)]
    + [("bx", d, t) for t in (1, 2) for d in (0, 1)]
)
W_ID = {(h,) + key: h * len(W_KEYS) + n for h in range(HEADS) for n, key in enumerate(W_KEYS)}
Y_KEYS = ("p1", "m1", "p2", "m2", "own", "fp1", "fm1", "f2")
Y_ID = {(g, key): len(W_ID) + g * len(Y_KEYS) + n for g in range(NX) for n, key in enumerate(Y_KEYS)}
N_MSG = len(W_ID) + len(Y_ID)


def iota(shape, dim):
    return lax.broadcasted_iota(jnp.int32, shape, dim)


def one_hot(mask):
    return jnp.where(mask, 1.0, 0.0).astype(BF16)


def kernel(
    tub, keep, row, slot, seg, gain, wq, wk, wv, out,
    xn, snd, rcv, nrm, wall, qkv, att, bias, place, present,
    lsem, a2a_s, a2a_r, ss, rs,
):
    p_me, j_me = lax.axis_index("dp"), lax.axis_index("tensor")
    x, z = p_me // NZ, lax.rem(p_me, NZ)
    y, c = j_me // 2, lax.rem(j_me, 2)

    def wrap(v, n):
        return lax.rem(v + n, n)

    def dp_of(xx, zz):
        return {"dp": wrap(xx, NX) * NZ + wrap(zz, NZ)}

    def ten_of(yy, cc):
        return {"tensor": wrap(yy, NY) * 2 + cc}

    barrier = pltpu.get_barrier_semaphore()

    @pl.loop(1, NDP)
    def _(d):
        pl.semaphore_signal(
            barrier, inc=1, device_id={"dp": lax.rem(p_me + d, NDP)}, device_id_type=MESH
        )

    for dev in (ten_of(y + 1, c), ten_of(y - 1, c), ten_of(y, 1 - c)):
        pl.semaphore_signal(barrier, inc=1, device_id=dev, device_id_type=MESH)

    local = []
    for h in range(HEADS):
        for n, w in enumerate((wq, wk, wv)):
            cp = pltpu.make_async_copy(
                w.at[:, pl.ds(h * HS, HS)],
                wall.at[h, x, z, :, pl.ds(n * HS, HS)],
                lsem.at[h * 3 + n],
            )
            cp.start()
            local.append(cp)

    @pl.loop(0, BLK // 16)
    def _(i):
        at = pl.ds(pl.multiple_of(i * 16, 16), 16)
        v = tub[at, :].astype(F32)
        v = v - jnp.mean(v, axis=-1, keepdims=True)
        var = jnp.mean(v * v, axis=-1, keepdims=True)
        xn[at, :] = (v * lax.rsqrt(var + 1e-06) * gain[...].astype(F32)).astype(BF16)

    pl.semaphore_wait(barrier, NDP - 1 + 3)
    for cp in local:
        cp.wait()

    sent = []

    def copy(region, n, dev):
        return pltpu.make_async_remote_copy(
            src_ref=region, dst_ref=region, send_sem=ss.at[n], recv_sem=rs.at[n],
            device_id=dev, device_id_type=MESH,
        )

    def send(region, n, dev):
        cp = copy(region, n, dev)
        cp.start()
        sent.append(cp)

    def recv(region, n):
        copy(region, n, dp_of(x + 1, z)).wait_recv()

    ALL = slice(None)
    a_rows, b_rows = (0, A_ROWS), (A_ROWS, B_ROWS)

    def halves(rows, plus):
        return ((rows[0], plus), (rows[0] + plus, rows[1] - plus))

    a_half = halves(a_rows, A_PLUS)
    bz_half, bx_half = halves(b_rows, BZ_PLUS), halves(b_rows, BX_PLUS)

    def wreg(h, xx, zz, rows):
        return wall.at[h, xx, zz, pl.ds(*rows), :]

    SIGN = (1, -1)

    class Ring:
        def __init__(self, name, h, axis, rows, cut, wide):
            self.name, self.h, self.axis = name, h, axis
            self.rows, self.cut, self.wide = rows, cut, wide
            self.far = (NX if axis == "x" else NZ) // 2

        def dev(self, d):
            return dp_of(x + SIGN[d], z) if self.axis == "x" else dp_of(x, z + SIGN[d])

        def region(self, d, t):
            rows = self.cut[d] if t == self.far else self.rows
            if self.axis == "x":
                return wreg(self.h, wrap(x - SIGN[d] * t, NX), ALL if self.wide else z, rows)
            return wreg(self.h, ALL if self.wide else x, wrap(z - SIGN[d] * t, NZ), rows)

        def begin(self):
            for d in (0, 1):
                send(self.region(d, 0), W_ID[self.h, self.name, d, 1], self.dev(d))

        def step(self, t):
            for d in (0, 1):
                recv(self.region(d, t), W_ID[self.h, self.name, d, t])
                if t < self.far:
                    hop = self.region(d, t)
                    if t + 1 == self.far:
                        rows = self.cut[d]
                        if self.axis == "x":
                            hop = wreg(self.h, wrap(x - SIGN[d] * t, NX), ALL if self.wide else z, rows)
                        else:
                            hop = wreg(self.h, ALL if self.wide else x, wrap(z - SIGN[d] * t, NZ), rows)
                    send(hop, W_ID[self.h, self.name, d, t + 1], self.dev(d))

    AX = [Ring("ax", h, "x", a_rows, a_half, False) for h in range(HEADS)]
    BZ = [Ring("bz", h, "z", b_rows, bz_half, False) for h in range(HEADS)]
    AZ = [Ring("az", h, "z", a_rows, a_half, True) for h in range(HEADS)]
    BX = [Ring("bx", h, "x", b_rows, bx_half, True) for h in range(HEADS)]

    for h in range(HEADS):
        BZ[h].begin()
        AX[h].begin()

    kept = [keep[e : e + 1, :] >= 0 for e in range(KEEP)]
    mine = [keep[e : e + 1, :] - j_me * KEEP for e in range(KEEP)]
    slots = [slot[e : e + 1, :] for e in range(KEEP)]
    target = []
    for e in range(KEEP):
        rank = jnp.zeros((1, NDP), jnp.int32)
        for f in range(KEEP):
            if f != e:
                rank = rank + jnp.where(kept[f] & (slots[f] < slots[e]), 1, 0)
        target.append(row[e : e + 1, :] * KEEP + rank + 1)
    flat = jnp.zeros((8, BLK), F32)
    for t in range(KEEP):
        aim = jnp.zeros((1, NDP), jnp.int32)
        for e in range(KEEP):
            aim = aim + jnp.where(kept[e] & (mine[e] == t), target[e], 0)
        spread = one_hot(iota((NDP, BLK), 1) == iota((NDP, BLK), 0) * KEEP + t)
        aim = jnp.broadcast_to(aim.astype(F32), (8, NDP)).astype(BF16)
        flat = flat + jnp.dot(aim, spread, preferred_element_type=F32)
    flat = flat[0:1, :].astype(jnp.int32) - 1
    r_id = iota((512, BLK), 0)
    hit = ((r_id >> 4) * KEEP + (r_id & 3)) == flat
    pick = jnp.concatenate([one_hot(hit & (((r_id >> 2) & 3) == q)) for q in range(4)], axis=1)
    for n in range(4):
        cols = jnp.concatenate(
            [xn[:, q * 1024 + n * 256 : q * 1024 + (n + 1) * 256] for q in range(4)], axis=0
        )
        moved = jnp.dot(pick, cols, preferred_element_type=F32).astype(BF16)
        snd[:, :, n * 256 : (n + 1) * 256] = moved.reshape(NDP, 16, 256)

    ORDER = (0, 1, 3, 2)
    for dx in ORDER:
        if dx == 0:
            pltpu.make_async_copy(snd.at[p_me], rcv.at[p_me], a2a_r.at[x]).start()

        @pl.loop(1 if dx == 0 else 0, NZ)
        def _(dz):
            dev = dp_of(x + dx, z + dz)
            pltpu.make_async_remote_copy(
                src_ref=snd.at[dev["dp"]], dst_ref=rcv.at[p_me], send_sem=a2a_s,
                recv_sem=a2a_r.at[x], device_id=dev, device_id_type=MESH,
            ).start()

    s_id, l_id = iota((BLK, BLK), 0), iota((BLK, BLK), 1)
    lanes = l_id.astype(F32)
    for j in range(NT):
        across = seg[:, j * BLK : (j + 1) * BLK].astype(F32)
        down = jnp.sum(jnp.where(s_id == l_id, across, 0.0), axis=1, keepdims=True)
        rank = jnp.sum(jnp.where((down == across) & (l_id < s_id), 1.0, 0.0), axis=1, keepdims=True)
        aim = jnp.where(down >= 0, jnp.floor(down * (1.0 / 32.0)) * KEEP + rank, -1.0)
        hit = jnp.where(aim == lanes, 1.0, 0.0)
        place[j] = hit.astype(BF16)
        present[j : j + 1, :] = jnp.sum(hit, axis=0, keepdims=True)
    wide = iota((BLK, 8 * BLK), 1)
    spread = one_hot(iota((BLK, 8 * BLK), 0) == (wide >> 7) * 16 + (wide & 15))
    valid = jnp.dot(present[...].astype(BF16), spread, preferred_element_type=F32)
    pick_j = ((iota((NT, 8 * BLK), 1) & 127) >> 4) == iota((NT, 8 * BLK), 0)
    valid = jnp.sum(jnp.where(pick_j, valid, 0.0), axis=0, keepdims=True)
    same = ((s_id & 15) >> 2) == ((l_id & 15) >> 2)
    for pg in range(8):
        live = same & (valid[:, pg * BLK : (pg + 1) * BLK] > 0.5)
        bias[pg] = jnp.where(live, 0.0, -1e30)

    o_id, i_id = iota((BLK, BLK), 0), iota((BLK, BLK), 1)
    src = ((o_id & 31) >> 2) * 16 + (o_id >> 5) * 4 + (o_id & 3)
    unpick = one_hot(i_id == src)

    def nreg(j, g, half=None):
        if half is None:
            return nrm.at[j, pl.ds(pl.multiple_of(g * 32, 32), 32), :]
        return nrm.at[j, pl.ds(pl.multiple_of(g * 32 + half * 16, 16), 16), :]

    up, down_, twin = ten_of(y + 1, c), ten_of(y - 1, c), ten_of(y, 1 - c)

    def jdx(yy, cc):
        return wrap(yy, NY) * 2 + cc

    def y_unpack(dx):
        g = wrap(x - dx, NX)
        group = rcv.at[pl.ds(pl.multiple_of(g * NZ, NZ), NZ)]
        pltpu.make_async_copy(group, group, a2a_r.at[g]).wait()
        got = rcv[pl.ds(pl.multiple_of(g * NZ, NZ), NZ)].reshape(BLK, 1024)
        back = jnp.dot(unpick, got, preferred_element_type=F32).astype(BF16)
        at = pl.ds(pl.multiple_of(g * 32, 32), 32)
        for q in range(4):
            nrm[j_me, at, q * 1024 : (q + 1) * 1024] = back[q * 32 : (q + 1) * 32, :]
        own = nreg(j_me, g)
        send(own, Y_ID[dx, "p1"], up)
        send(own, Y_ID[dx, "m1"], down_)
        send(own, Y_ID[dx, "own"], twin)

    def y_near(dx):
        g = wrap(x - dx, NX)
        lo, hi = jdx(y - 1, c), jdx(y + 1, c)
        recv(nreg(lo, g), Y_ID[dx, "p1"])
        send(nreg(lo, g, 0), Y_ID[dx, "p2"], up)
        send(nreg(lo, g), Y_ID[dx, "fp1"], twin)
        recv(nreg(hi, g), Y_ID[dx, "m1"])
        send(nreg(hi, g, 1), Y_ID[dx, "m2"], down_)
        send(nreg(hi, g), Y_ID[dx, "fm1"], twin)

    def y_far(dx):
        g = wrap(x - dx, NX)
        far = jdx(y + 2, c)
        recv(nreg(far, g, 0), Y_ID[dx, "p2"])
        recv(nreg(far, g, 1), Y_ID[dx, "m2"])
        send(nreg(far, g), Y_ID[dx, "f2"], twin)

    def y_end(dx):
        g = wrap(x - dx, NX)
        recv(nreg(jdx(y, 1 - c), g), Y_ID[dx, "own"])
        recv(nreg(jdx(y - 1, 1 - c), g), Y_ID[dx, "fp1"])
        recv(nreg(jdx(y + 1, 1 - c), g), Y_ID[dx, "fm1"])
        recv(nreg(jdx(y + 2, 1 - c), g), Y_ID[dx, "f2"])

    def e(n, h):
        if n == 1:
            BZ[h].step(1)
            AX[h].step(1)
        elif n == 2:
            BZ[h].step(2)
            AX[h].step(2)
            AZ[h].begin()
        elif n == 3:
            BZ[h].step(3)
        else:
            BZ[h].step(4)
            BX[h].begin()

    def f(n, h):
        if n == 4:
            BX[h].step(1)
        elif n == 6:
            BX[h].step(2)
        else:
            AZ[h].step({1: 1, 2: 2, 3: 3, 5: 4}[n])

    def qkv_of(h):
        @pl.loop(0, NT // 2)
        def _(m):
            lhs = nrm[pl.ds(m * 2, 2)].reshape(2 * BLK, NDP * BLK)
            rhs = wall[h].reshape(NDP * BLK, 3 * HS)
            acc = jnp.dot(lhs, rhs, preferred_element_type=F32)
            col = iota(acc.shape, 1)
            acc = acc * jnp.where(col < HS, HS ** (-0.5), 1.0)
            qkv[pl.ds(m * 2, 2)] = acc.astype(BF16).reshape(2, BLK, 3 * HS)

    def attend(h):
        for pg in range(8):
            part = qkv[:, pg * 16 : (pg + 1) * 16, :].reshape(BLK, 3 * HS)
            q, k, v = part[:, :HS], part[:, HS : 2 * HS], part[:, 2 * HS :]
            s = lax.dot_general(q, k, (((1,), (1,)), ((), ())), preferred_element_type=F32)
            s = s + bias[pg]
            s = jnp.exp(s - jnp.max(s, axis=1, keepdims=True))
            w = (s / jnp.sum(s, axis=1, keepdims=True)).astype(BF16)
            o = jnp.dot(w, v, preferred_element_type=F32).astype(BF16)
            att[:, pg * 16 : (pg + 1) * 16, h * HS : (h + 1) * HS] = o.reshape(NT, 16, HS)

    e(1, 0)
    e(1, 1)
    e(2, 0)
    e(1, 2)
    e(2, 1)
    y_unpack(0)
    e(3, 0)
    e(2, 2)
    e(3, 1)
    e(4, 0)
    y_unpack(1)
    f(1, 0)
    e(3, 2)
    e(4, 1)
    y_near(0)
    f(2, 0)
    f(1, 1)
    e(4, 2)
    y_unpack(3)
    f(3, 0)
    f(2, 1)
    f(1, 2)
    y_far(0)
    y_near(1)
    f(4, 0)
    f(3, 1)
    f(2, 2)
    y_unpack(2)
    f(5, 0)
    f(3, 2)
    y_far(1)
    y_near(3)
    f(5, 1)
    f(4, 1)
    f(5, 2)
    y_far(3)
    y_near(2)
    y_far(2)
    f(6, 0)
    f(4, 2)
    for dx in ORDER:
        y_end(dx)
    f(6, 1)
    f(6, 2)

    for h in range(HEADS):
        qkv_of(h)
        attend(h)
    for j in range(NT):
        out[j * BLK : (j + 1) * BLK, :] = jnp.dot(
            place[j], att[j], preferred_element_type=F32
        ).astype(BF16)

    for cp in sent:
        cp.wait_send()
    most = snd.at[pl.ds(0, NDP - 1)]
    pltpu.make_async_copy(most, most, a2a_s).wait()


def body(tubelets, keep_index, dest_row, dest_slot, segment, ln_gain, w_query, w_key, w_value):
    width = tubelets.shape[2]
    vmem = pl.BlockSpec(memory_space=pltpu.VMEM)
    hbm = pl.BlockSpec(memory_space=pl.ANY)
    dma = pltpu.SemaphoreType.DMA
    cols = w_query.shape[1]
    mixed = pl.pallas_call(
        kernel,
        out_shape=jax.ShapeDtypeStruct((NT * BLK, cols), BF16),
        in_specs=[vmem] * 6 + [hbm] * 3,
        out_specs=vmem,
        scratch_shapes=[
            pltpu.VMEM((BLK, width), BF16),
            pltpu.VMEM((NDP, 16, width // 4), BF16),
            pltpu.VMEM((NDP, 16, width // 4), BF16),
            pltpu.VMEM((NT, BLK, width), BF16),
            pltpu.VMEM((HEADS, NX, NZ, BLK, 3 * HS), BF16),
            pltpu.VMEM((NT, BLK, 3 * HS), BF16),
            pltpu.VMEM((NT, BLK, cols), BF16),
            pltpu.VMEM((8, BLK, BLK), F32),
            pltpu.VMEM((NT, BLK, BLK), BF16),
            pltpu.VMEM((NT, BLK), F32),
            dma((3 * HEADS,)),
            dma,
            dma((NX,)),
            dma((N_MSG,)),
            dma((N_MSG,)),
        ],
        compiler_params=pltpu.CompilerParams(
            collective_id=0, has_side_effects=True, vmem_limit_bytes=60 * 1024 * 1024
        ),
        name="repack_attend",
    )(
        tubelets.reshape(BLK, width),
        keep_index.T,
        dest_row.T,
        dest_slot.T,
        segment,
        ln_gain.reshape(1, width),
        w_query,
        w_key,
        w_value,
    )
    return mixed.reshape(1, NT * BLK, cols)


def solution(mesh):
    return jax.shard_map(
        body,
        mesh=mesh,
        in_specs=(
            P("dp", "tensor", None),
            P("dp", "tensor"),
            P("dp", "tensor"),
            P("dp", "tensor"),
            P("dp", None),
            P(),
            P("dp", "tensor"),
            P("dp", "tensor"),
            P("dp", "tensor"),
        ),
        out_specs=P("dp", None, "tensor"),
        check_vma=False,
    )
```

```python
import jax
import jax.numpy as jnp
from jax import lax
from jax.experimental import pallas as pl
from jax.experimental.pallas import tpu as pltpu
from jax.sharding import PartitionSpec as P

MESH = pl.DeviceIdType.MESH
F32 = jnp.float32
BF16 = jnp.bfloat16
HS = 128
NX, NZ, NY = 4, 8, 4
NDP, NT = NX * NZ, 2 * NY
KEEP = 4
HEADS = 3
BLK = 128

A_ROWS, A_PLUS = 32, 16
B_ROWS = BLK - A_ROWS
BZ_PLUS, BX_PLUS = 48, 48

SHIFTS = (0, 1, -1, 2, -2, 3, -3, 4)

W_KEYS = (
    [("ax", d, t) for t in (1, 2) for d in (0, 1)]
    + [("bz", d, t) for t in (1, 2, 3, 4) for d in (0, 1)]
    + [("az", d, t) for t in (1, 2, 3, 4) for d in (0, 1)]
    + [(("bx", s), d, t) for s in SHIFTS for t in (1, 2) for d in (0, 1)]
)
W_ID = {(h,) + key: h * len(W_KEYS) + n for h in range(HEADS) for n, key in enumerate(W_KEYS)}
Y_KEYS = ("p1", "m1", "p2", "m2", "own", "fp1", "fm1", "f2")
Y_ID = {(g, key): len(W_ID) + g * len(Y_KEYS) + n for g in range(NX) for n, key in enumerate(Y_KEYS)}
N_MSG = len(W_ID) + len(Y_ID)

PLAN = (
    ("ax", 0, 1), ("bz", 0, 1), ("bx", 0, 0, 1), ("ax", 1, 1), ("bz", 1, 1), ("bx", 1, 0, 1), ("ax", 0, 2),
    ("bx", 0, 1, 1), ("bx", 0, -1, 1), ("bx", 0, 0, 2), ("ax", 1, 2), ("yu", 0), ("A", 3), ("A", 2),
    ("bx", 1, 1, 1), ("bz", 0, 2), ("bx", 1, -1, 1), ("bx", 1, 0, 2), ("bx", 0, 1, 2), ("yu", 1), ("bz", 1, 2),
    ("bx", 0, -1, 2), ("az", 0, 1), ("yn", 0), ("pl",), ("yn", 1), ("bx", 1, 1, 2), ("bx", 0, 2, 1), ("yf", 0),
    ("yu", 3), ("bx", 0, -2, 1), ("bx", 1, -1, 2), ("ye", 0), ("bx", 1, 2, 1), ("yf", 1), ("az", 1, 1),
    ("bx", 1, -2, 1), ("bx", 0, 2, 2), ("ye", 1), ("bx", 0, -2, 2), ("bz", 0, 3), ("bx", 1, 2, 2),
    ("bx", 1, -2, 2), ("yu", 2), ("bz", 1, 3), ("yn", 3), ("bx", 0, 3, 1), ("az", 0, 2), ("bx", 0, -3, 1),
    ("bx", 1, 3, 1), ("az", 1, 2), ("bz", 0, 4), ("W", 2), ("bx", 1, -3, 1), ("bz", 1, 4), ("bx", 0, 3, 2),
    ("yn", 2), ("bx", 0, -3, 2), ("bx", 1, 3, 2), ("az", 0, 3), ("bx", 0, 4, 1), ("yf", 3), ("ax", 2, 1),
    ("az", 1, 3), ("bx", 2, 0, 1), ("bz", 2, 1), ("ye", 3), ("bx", 1, -3, 2), ("yf", 2), ("az", 0, 4),
    ("bx", 1, 4, 1), ("az", 1, 4), ("bx", 0, 4, 2), ("ax", 2, 2), ("ye", 2), ("q", 0, 0), ("bx", 2, 0, 2),
    ("bz", 2, 2), ("bx", 2, 1, 1), ("q", 0, 1), ("az", 2, 1), ("bx", 2, -1, 1), ("bx", 1, 4, 2),
    ("bx", 2, 2, 1), ("bz", 2, 3), ("t", 0), ("bx", 2, -2, 1), ("bx", 2, 1, 2), ("q", 1, 0), ("bx", 2, -1, 2),
    ("az", 2, 2), ("bx", 2, 2, 2), ("bz", 2, 4), ("bx", 2, 3, 1), ("q", 1, 1), ("bx", 2, -3, 1),
    ("bx", 2, -2, 2), ("t", 1), ("bx", 2, 4, 1), ("az", 2, 3), ("bx", 2, 3, 2), ("bx", 2, -3, 2),
    ("bx", 2, 4, 2), ("az", 2, 4), ("q", 2, 0), ("q", 2, 1), ("t", 2),
)


FIRST_GROUPS, FIRST_HEADS = (0, 1), (0, 1)


def iota(shape, dim):
    return lax.broadcasted_iota(jnp.int32, shape, dim)


def one_hot(mask):
    return jnp.where(mask, 1.0, 0.0).astype(BF16)


def kernel(
    tub_hbm, keep, row, slot, seg, gain, wq, wk, wv, out,
    tub, gains, xn, snd, rcv, nrm, wall, qkv, att, bias, place, present,
    lsem, a2a_s, a2a_r, ss, rs, entered,
):
    width = xn.shape[1]
    p_me, j_me = lax.axis_index("dp"), lax.axis_index("tensor")
    x, z = p_me // NZ, lax.rem(p_me, NZ)
    y, c = j_me // 2, lax.rem(j_me, 2)

    def wrap(v, n):
        return lax.rem(v + n, n)

    def dp_of(xx, zz):
        return {"dp": wrap(xx, NX) * NZ + wrap(zz, NZ)}

    def ten_of(yy, cc):
        return {"tensor": wrap(yy, NY) * 2 + cc}

    barrier = pltpu.get_barrier_semaphore()
    near = [dp_of(x + d, z) for d in range(1, NX)]
    peers = near + [dp_of(x, z + d) for d in range(1, NZ)]
    peers += [ten_of(y + 1, c), ten_of(y - 1, c), ten_of(y, 1 - c)]
    for dev in peers:
        pl.semaphore_signal(barrier, inc=1, device_id=dev, device_id_type=MESH)

    load = pltpu.make_async_copy(tub_hbm, tub, lsem.at[3 * HEADS])
    load.start()

    local = []
    for h in range(HEADS):
        for n, w in enumerate((wq, wk, wv)):
            cp = pltpu.make_async_copy(
                w.at[:, pl.ds(h * HS, HS)],
                wall.at[h, x, z, :, pl.ds(n * HS, HS)],
                lsem.at[h * 3 + n],
            )
            cp.start()
            local.append(cp)

    for n in range(width // BLK):
        gains[:, n * BLK : (n + 1) * BLK] = jnp.broadcast_to(gain[n : n + 1, :].astype(F32), (8, BLK))

    load.wait()
    for t in range(KEEP):
        v = tub[:, t, :].astype(F32)
        v = v - jnp.mean(v, axis=-1, keepdims=True)
        var = jnp.mean(v * v, axis=-1, keepdims=True)
        xn[t * NDP : (t + 1) * NDP, :] = (v * lax.rsqrt(var + 1e-06) * gains[0:1, :]).astype(BF16)

    pl.semaphore_wait(barrier, len(peers))
    for dev in near:
        pl.semaphore_signal(entered, inc=1, device_id=dev, device_id_type=MESH)
    for cp in local:
        cp.wait()

    sent = []

    def copy(region, n, dev):
        return pltpu.make_async_remote_copy(
            src_ref=region, dst_ref=region, send_sem=ss.at[n], recv_sem=rs.at[n],
            device_id=dev, device_id_type=MESH,
        )

    def send(region, n, dev):
        cp = copy(region, n, dev)
        cp.start()
        sent.append(cp)

    def recv(region, n):
        copy(region, n, dp_of(x + 1, z)).wait_recv()

    ALL = slice(None)
    a_rows, b_rows = (0, A_ROWS), (A_ROWS, B_ROWS)

    def halves(rows, plus):
        return ((rows[0], plus), (rows[0] + plus, rows[1] - plus))

    a_half = halves(a_rows, A_PLUS)
    bz_half, bx_half = halves(b_rows, BZ_PLUS), halves(b_rows, BX_PLUS)

    def wreg(h, xx, zz, rows):
        return wall.at[h, xx, zz, pl.ds(*rows), :]

    SIGN = (1, -1)

    class Ring:
        def __init__(self, name, h, axis, rows, cut, wide, zz=z):
            self.name, self.h, self.axis = name, h, axis
            self.rows, self.cut, self.wide, self.zz = rows, cut, wide, zz
            self.far = (NX if axis == "x" else NZ) // 2

        def dev(self, d):
            return dp_of(x + SIGN[d], z) if self.axis == "x" else dp_of(x, z + SIGN[d])

        def region(self, d, t):
            rows = self.cut[d] if t == self.far else self.rows
            if self.axis == "x":
                return wreg(self.h, wrap(x - SIGN[d] * t, NX), self.zz, rows)
            return wreg(self.h, ALL if self.wide else x, wrap(z - SIGN[d] * t, NZ), rows)

        def begin(self):
            for d in (0, 1):
                send(self.region(d, 0), W_ID[self.h, self.name, d, 1], self.dev(d))

        def step(self, t):
            for d in (0, 1):
                recv(self.region(d, t), W_ID[self.h, self.name, d, t])
                if t < self.far:
                    hop = self.region(d, t)
                    if t + 1 == self.far:
                        rows = self.cut[d]
                        if self.axis == "x":
                            hop = wreg(self.h, wrap(x - SIGN[d] * t, NX), self.zz, rows)
                        else:
                            hop = wreg(self.h, ALL if self.wide else x, wrap(z - SIGN[d] * t, NZ), rows)
                    send(hop, W_ID[self.h, self.name, d, t + 1], self.dev(d))

    AX = [Ring("ax", h, "x", a_rows, a_half, False) for h in range(HEADS)]
    BZ = [Ring("bz", h, "z", b_rows, bz_half, False) for h in range(HEADS)]
    AZ = [Ring("az", h, "z", a_rows, a_half, True) for h in range(HEADS)]
    BX = [
        {s: Ring(("bx", s), h, "x", b_rows, bx_half, False, wrap(z - s, NZ)) for s in SHIFTS}
        for h in range(HEADS)
    ]

    def begin(h):
        BZ[h].begin()
        AX[h].begin()
        BX[h][0].begin()

    for h in FIRST_HEADS:
        begin(h)

    kept = [keep[e : e + 1, :] >= 0 for e in range(KEEP)]
    mine = [keep[e : e + 1, :] - j_me * KEEP for e in range(KEEP)]
    slots = [slot[e : e + 1, :] for e in range(KEEP)]
    target = []
    for e in range(KEEP):
        rank = jnp.zeros((1, NDP), jnp.int32)
        for f in range(KEEP):
            if f != e:
                rank = rank + jnp.where(kept[f] & (slots[f] < slots[e]), 1, 0)
        target.append(row[e : e + 1, :] * KEEP + rank + 1)
    aims = []
    for t in range(KEEP):
        aim = jnp.zeros((1, NDP), jnp.int32)
        for e in range(KEEP):
            aim = aim + jnp.where(kept[e] & (mine[e] == t), target[e], 0)
        aims.append(aim)
    flat = jnp.concatenate(aims, axis=1) - 1
    r_id = iota((512, BLK), 0)
    hit = ((r_id >> 4) * KEEP + (r_id & 3)) == flat
    pick = jnp.concatenate([one_hot(hit & (((r_id >> 2) & 3) == q)) for q in range(4)], axis=1)
    for n in range(4):
        cols = jnp.concatenate(
            [xn[:, q * 1024 + n * 256 : q * 1024 + (n + 1) * 256] for q in range(4)], axis=0
        )
        moved = jnp.dot(pick, cols, preferred_element_type=F32).astype(BF16)
        snd[:, :, n * 256 : (n + 1) * 256] = moved.reshape(NDP, 16, 256)

    pl.semaphore_wait(entered, len(near))

    def exchange(dx):
        if dx == 0:
            pltpu.make_async_copy(snd.at[p_me], rcv.at[p_me], a2a_r.at[x]).start()

        @pl.loop(1 if dx == 0 else 0, NZ)
        def _(dz):
            dev = dp_of(x + dx, z + dz)
            pltpu.make_async_remote_copy(
                src_ref=snd.at[dev["dp"]], dst_ref=rcv.at[p_me], send_sem=a2a_s,
                recv_sem=a2a_r.at[x], device_id=dev, device_id_type=MESH,
            ).start()

    for dx in FIRST_GROUPS:
        exchange(dx)

    s_id, l_id = iota((BLK, BLK), 0), iota((BLK, BLK), 1)
    lanes = l_id.astype(F32)

    def slot_order():
        for j in range(NT):
            across = seg[:, j * BLK : (j + 1) * BLK].astype(F32)
            down = jnp.sum(jnp.where(s_id == l_id, across, 0.0), axis=1, keepdims=True)
            rank = jnp.sum(jnp.where((down == across) & (l_id < s_id), 1.0, 0.0), axis=1, keepdims=True)
            aim = jnp.where(down >= 0, jnp.floor(down * (1.0 / 32.0)) * KEEP + rank, -1.0)
            hit = jnp.where(aim == lanes, 1.0, 0.0)
            place[j] = hit.astype(BF16)
            present[j : j + 1, :] = jnp.sum(hit, axis=0, keepdims=True)
        wide = iota((BLK, 8 * BLK), 1)
        spread = one_hot(iota((BLK, 8 * BLK), 0) == (wide >> 7) * 16 + (wide & 15))
        valid = jnp.dot(present[...].astype(BF16), spread, preferred_element_type=F32)
        pick_j = ((iota((NT, 8 * BLK), 1) & 127) >> 4) == iota((NT, 8 * BLK), 0)
        valid = jnp.sum(jnp.where(pick_j, valid, 0.0), axis=0, keepdims=True)
        same = ((s_id & 15) >> 2) == ((l_id & 15) >> 2)
        for pg in range(8):
            live = same & (valid[:, pg * BLK : (pg + 1) * BLK] > 0.5)
            bias[pg] = jnp.where(live, 0.0, -1e30)

    o_id, i_id = iota((BLK, BLK), 0), iota((BLK, BLK), 1)
    src = ((o_id & 31) >> 2) * 16 + (o_id >> 5) * 4 + (o_id & 3)
    unpick = one_hot(i_id == src)

    def nreg(j, g, half=None):
        if half is None:
            return nrm.at[j, pl.ds(pl.multiple_of(g * 32, 32), 32), :]
        return nrm.at[j, pl.ds(pl.multiple_of(g * 32 + half * 16, 16), 16), :]

    up, down_, twin = ten_of(y + 1, c), ten_of(y - 1, c), ten_of(y, 1 - c)

    def jdx(yy, cc):
        return wrap(yy, NY) * 2 + cc

    def y_unpack(dx):
        g = wrap(x - dx, NX)
        group = rcv.at[pl.ds(pl.multiple_of(g * NZ, NZ), NZ)]
        pltpu.make_async_copy(group, group, a2a_r.at[g]).wait()
        got = rcv[pl.ds(pl.multiple_of(g * NZ, NZ), NZ)].reshape(BLK, 1024)
        back = jnp.dot(unpick, got, preferred_element_type=F32).astype(BF16)
        at = pl.ds(pl.multiple_of(g * 32, 32), 32)
        for q in range(4):
            nrm[j_me, at, q * 1024 : (q + 1) * 1024] = back[q * 32 : (q + 1) * 32, :]
        own = nreg(j_me, g)
        send(own, Y_ID[dx, "p1"], up)
        send(own, Y_ID[dx, "m1"], down_)
        send(own, Y_ID[dx, "own"], twin)

    def y_near(dx):
        g = wrap(x - dx, NX)
        lo, hi = jdx(y - 1, c), jdx(y + 1, c)
        recv(nreg(lo, g), Y_ID[dx, "p1"])
        send(nreg(lo, g, 0), Y_ID[dx, "p2"], up)
        send(nreg(lo, g), Y_ID[dx, "fp1"], twin)
        recv(nreg(hi, g), Y_ID[dx, "m1"])
        send(nreg(hi, g, 1), Y_ID[dx, "m2"], down_)
        send(nreg(hi, g), Y_ID[dx, "fm1"], twin)

    def y_far(dx):
        g = wrap(x - dx, NX)
        far = jdx(y + 2, c)
        recv(nreg(far, g, 0), Y_ID[dx, "p2"])
        recv(nreg(far, g, 1), Y_ID[dx, "m2"])
        send(nreg(far, g), Y_ID[dx, "f2"], twin)

    def y_end(dx):
        g = wrap(x - dx, NX)
        recv(nreg(jdx(y, 1 - c), g), Y_ID[dx, "own"])
        recv(nreg(jdx(y - 1, 1 - c), g), Y_ID[dx, "fp1"])
        recv(nreg(jdx(y + 1, 1 - c), g), Y_ID[dx, "fm1"])
        recv(nreg(jdx(y + 2, 1 - c), g), Y_ID[dx, "f2"])

    def weights(name, h, *at):
        if name == "bx":
            BX[h][at[0]].step(at[1])
            return
        t = at[0]
        {"ax": AX, "bz": BZ, "az": AZ}[name][h].step(t)
        if name == "ax" and t == 2:
            AZ[h].begin()
        if name == "bz":
            for s in (t, -t) if t < 4 else (t,):
                BX[h][s].begin()

    def qkv_of(h, half):
        @pl.loop(half * 2, half * 2 + 2)
        def _(m):
            lhs = nrm[pl.ds(m * 2, 2)].reshape(2 * BLK, NDP * BLK)
            rhs = wall[h].reshape(NDP * BLK, 3 * HS)
            acc = jnp.dot(lhs, rhs, preferred_element_type=F32)
            col = iota(acc.shape, 1)
            acc = acc * jnp.where(col < HS, HS ** (-0.5), 1.0)
            qkv[pl.ds(m * 2, 2)] = acc.astype(BF16).reshape(2, BLK, 3 * HS)

    def attend(h):
        for pg in range(8):
            part = qkv[:, pg * 16 : (pg + 1) * 16, :].reshape(BLK, 3 * HS)
            q, k, v = part[:, :HS], part[:, HS : 2 * HS], part[:, 2 * HS :]
            s = lax.dot_general(q, k, (((1,), (1,)), ((), ())), preferred_element_type=F32)
            s = s + bias[pg]
            s = jnp.exp(s - jnp.max(s, axis=1, keepdims=True))
            w = (s / jnp.sum(s, axis=1, keepdims=True)).astype(BF16)
            o = jnp.dot(w, v, preferred_element_type=F32).astype(BF16)
            att[:, pg * 16 : (pg + 1) * 16, h * HS : (h + 1) * HS] = o.reshape(NT, 16, HS)

    acts = {
        "yu": y_unpack, "yn": y_near, "yf": y_far, "ye": y_end, "A": exchange, "W": begin,
        "pl": slot_order, "q": qkv_of, "t": attend,
    }
    for name, *rest in PLAN:
        if name in acts:
            acts[name](*rest)
        else:
            weights(name, *rest)

    for j in range(NT):
        out[j * BLK : (j + 1) * BLK, :] = jnp.dot(
            place[j], att[j], preferred_element_type=F32
        ).astype(BF16)

    for cp in sent:
        cp.wait_send()
    most = snd.at[pl.ds(0, NDP - 1)]
    pltpu.make_async_copy(most, most, a2a_s).wait()


def body(tubelets, keep_index, dest_row, dest_slot, segment, ln_gain, w_query, w_key, w_value):
    width = tubelets.shape[2]
    vmem = pl.BlockSpec(memory_space=pltpu.VMEM)
    hbm = pl.BlockSpec(memory_space=pl.ANY)
    dma = pltpu.SemaphoreType.DMA
    cols = w_query.shape[1]
    mixed = pl.pallas_call(
        kernel,
        out_shape=jax.ShapeDtypeStruct((NT * BLK, cols), BF16),
        in_specs=[hbm] + [vmem] * 5 + [hbm] * 3,
        out_specs=vmem,
        scratch_shapes=[
            pltpu.VMEM(tubelets.shape, BF16),
            pltpu.VMEM((8, width), F32),
            pltpu.VMEM((BLK, width), BF16),
            pltpu.VMEM((NDP, 16, width // 4), BF16),
            pltpu.VMEM((NDP, 16, width // 4), BF16),
            pltpu.VMEM((NT, BLK, width), BF16),
            pltpu.VMEM((HEADS, NX, NZ, BLK, 3 * HS), BF16),
            pltpu.VMEM((NT, BLK, 3 * HS), BF16),
            pltpu.VMEM((NT, BLK, cols), BF16),
            pltpu.VMEM((8, BLK, BLK), F32),
            pltpu.VMEM((NT, BLK, BLK), BF16),
            pltpu.VMEM((NT, BLK), F32),
            dma((3 * HEADS + 1,)),
            dma,
            dma((NX,)),
            dma((N_MSG,)),
            dma((N_MSG,)),
            pltpu.SemaphoreType.REGULAR,
        ],
        compiler_params=pltpu.CompilerParams(
            collective_id=0, has_side_effects=True, vmem_limit_bytes=60 * 1024 * 1024
        ),
        name="repack_attend",
    )(
        tubelets,
        keep_index.T,
        dest_row.T,
        dest_slot.T,
        segment,
        ln_gain.reshape(width // BLK, BLK),
        w_query,
        w_key,
        w_value,
    )
    return mixed.reshape(1, NT * BLK, cols)


def solution(mesh):
    return jax.shard_map(
        body,
        mesh=mesh,
        in_specs=(
            P("dp", "tensor", None),
            P("dp", "tensor"),
            P("dp", "tensor"),
            P("dp", "tensor"),
            P("dp", None),
            P(),
            P("dp", "tensor"),
            P("dp", "tensor"),
            P("dp", "tensor"),
        ),
        out_specs=P("dp", None, "tensor"),
        check_vma=False,
    )
```

```python
import jax
import jax.numpy as jnp
from jax import lax
from jax.experimental import pallas as pl
from jax.experimental.pallas import tpu as pltpu
from jax.sharding import PartitionSpec as P

MESH = pl.DeviceIdType.MESH
F32 = jnp.float32
BF16 = jnp.bfloat16
HS = 128
NX, NZ, NY = 4, 8, 4
NDP, NT = NX * NZ, 2 * NY
KEEP = 4
HEADS = 3
BLK = 128

A_ROWS, A_PLUS = 32, 16
B_ROWS = BLK - A_ROWS
BZ_PLUS, BX_PLUS = 48, 48

SHIFTS = (0, 1, -1, 2, -2, 3, -3, 4)

W_KEYS = (
    [("ax", d, t) for t in (1, 2) for d in (0, 1)]
    + [("bz", d, t) for t in (1, 2, 3, 4) for d in (0, 1)]
    + [("az", d, t) for t in (1, 2, 3, 4) for d in (0, 1)]
    + [(("bx", s), d, t) for s in SHIFTS for t in (1, 2) for d in (0, 1)]
)
W_ID = {(h,) + key: h * len(W_KEYS) + n for h in range(HEADS) for n, key in enumerate(W_KEYS)}
Y_KEYS = ("p1", "m1", "p2", "m2", "own", "fp1", "fm1", "f2")
Y_ID = {(g, key): len(W_ID) + g * len(Y_KEYS) + n for g in range(NX) for n, key in enumerate(Y_KEYS)}
N_MSG = len(W_ID) + len(Y_ID)

PLAN = (
    ("ax", 0, 1), ("bz", 0, 1), ("A", 1), ("bx", 0, 0, 1), ("ax", 1, 1), ("bz", 1, 1), ("bx", 1, 0, 1),
    ("ax", 0, 2), ("bx", 0, 1, 1), ("bx", 0, -1, 1), ("bz", 0, 2), ("A", 3), ("bx", 0, 0, 2), ("ax", 1, 2),
    ("yu", 0), ("A", 2), ("bx", 1, 1, 1), ("bx", 1, -1, 1), ("y0", 0), ("bx", 1, 0, 2), ("bz", 1, 2),
    ("bx", 0, 1, 2), ("bx", 0, -1, 2), ("bx", 0, 2, 1), ("az", 0, 1), ("yn", 0), ("pl",), ("bx", 0, -2, 1),
    ("yu", 1), ("bz", 0, 3), ("y1", 0), ("y0", 1), ("yf", 0), ("bx", 1, 1, 2), ("y2", 0), ("bx", 1, -1, 2),
    ("bx", 1, 2, 1), ("yn", 1), ("yu", 3), ("bx", 1, -2, 1), ("bx", 0, 2, 2), ("bx", 0, -2, 2), ("y1", 1),
    ("bx", 0, 3, 1), ("az", 1, 1), ("y0", 3), ("yf", 1), ("bx", 0, -3, 1), ("bx", 1, 2, 2), ("bz", 1, 3),
    ("bx", 1, -2, 2), ("y2", 1), ("bx", 0, 3, 2), ("bx", 0, -3, 2), ("yu", 2), ("az", 0, 2), ("bz", 0, 4),
    ("W", 2), ("bx", 1, 3, 1), ("yn", 3), ("y0", 2), ("bx", 1, -3, 1), ("az", 1, 2), ("bz", 1, 4),
    ("bx", 0, 4, 1), ("ax", 2, 1), ("y1", 3), ("bx", 2, 0, 1), ("az", 0, 3), ("bx", 1, 3, 2), ("yn", 2),
    ("bx", 1, -3, 2), ("bz", 2, 1), ("bx", 1, 4, 1), ("bx", 0, 4, 2), ("az", 1, 3), ("ax", 2, 2), ("yf", 3),
    ("y1", 2), ("bx", 2, 0, 2), ("az", 0, 4), ("q", 0, 0, 0), ("q", 0, 0, 1), ("bx", 2, 1, 1), ("y2", 3),
    ("bz", 2, 2), ("yf", 2), ("q", 0, 0, 2), ("bx", 2, -1, 1), ("az", 1, 4), ("q", 1, 0, 0), ("bx", 1, 4, 2),
    ("bx", 2, 1, 2), ("y2", 2), ("q", 0, 0, 3), ("az", 2, 1), ("q", 0, 1), ("bx", 2, 2, 1), ("bz", 2, 3),
    ("bx", 2, -2, 1), ("t", 0), ("bx", 2, -1, 2), ("q", 1, 0, 1), ("az", 2, 2), ("bx", 2, 2, 2),
    ("q", 1, 0, 2), ("bz", 2, 4), ("q", 1, 0, 3), ("bx", 2, 3, 1), ("q", 1, 1), ("bx", 2, -3, 1), ("az", 2, 3),
    ("bx", 2, -2, 2), ("t", 1), ("bx", 2, 4, 1), ("bx", 2, 3, 2), ("az", 2, 4), ("q", 2, 0, 0),
    ("bx", 2, -3, 2), ("bx", 2, 4, 2), ("q", 2, 0, 1), ("q", 2, 0, 2), ("q", 2, 0, 3), ("q", 2, 1), ("t", 2),
)
FIRST_GROUPS, FIRST_HEADS = (0,), (0, 1)


def iota(shape, dim):
    return lax.broadcasted_iota(jnp.int32, shape, dim)


def one_hot(mask):
    return jnp.where(mask, 1.0, 0.0).astype(BF16)


def kernel(
    tub_hbm, keep, row, slot, seg, gain, wq, wk, wv, out,
    tub, gains, xn, snd, rcv, nrm, wall, acc, qkv, att, score, prob, bias, place, present,
    lsem, a2a_s, a2a_r, ss, rs, entered,
):
    width = xn.shape[1]
    p_me, j_me = lax.axis_index("dp"), lax.axis_index("tensor")
    x, z = p_me // NZ, lax.rem(p_me, NZ)
    y, c = j_me // 2, lax.rem(j_me, 2)

    def wrap(v, n):
        return lax.rem(v + n, n)

    def dp_of(xx, zz):
        return {"dp": wrap(xx, NX) * NZ + wrap(zz, NZ)}

    def ten_of(yy, cc):
        return {"tensor": wrap(yy, NY) * 2 + cc}

    barrier = pltpu.get_barrier_semaphore()
    near = [dp_of(x + d, z) for d in range(1, NX)]
    peers = near + [dp_of(x, z + d) for d in range(1, NZ)]
    peers += [ten_of(y + 1, c), ten_of(y - 1, c), ten_of(y, 1 - c)]
    for dev in peers:
        pl.semaphore_signal(barrier, inc=1, device_id=dev, device_id_type=MESH)

    load = pltpu.make_async_copy(tub_hbm, tub, lsem.at[3 * HEADS])
    load.start()

    local = []
    for h in range(HEADS):
        for n, w in enumerate((wq, wk, wv)):
            cp = pltpu.make_async_copy(
                w.at[:, pl.ds(h * HS, HS)],
                wall.at[h, x, z, :, pl.ds(n * HS, HS)],
                lsem.at[h * 3 + n],
            )
            cp.start()
            local.append(cp)

    pl.semaphore_wait(barrier, len(peers))
    for dev in near:
        pl.semaphore_signal(entered, inc=1, device_id=dev, device_id_type=MESH)
    for cp in local:
        cp.wait()

    sent = []

    def copy(region, n, dev):
        return pltpu.make_async_remote_copy(
            src_ref=region, dst_ref=region, send_sem=ss.at[n], recv_sem=rs.at[n],
            device_id=dev, device_id_type=MESH,
        )

    def send(region, n, dev):
        cp = copy(region, n, dev)
        cp.start()
        sent.append(cp)

    def recv(region, n):
        copy(region, n, dp_of(x + 1, z)).wait_recv()

    ALL = slice(None)
    a_rows, b_rows = (0, A_ROWS), (A_ROWS, B_ROWS)

    def halves(rows, plus):
        return ((rows[0], plus), (rows[0] + plus, rows[1] - plus))

    a_half = halves(a_rows, A_PLUS)
    bz_half, bx_half = halves(b_rows, BZ_PLUS), halves(b_rows, BX_PLUS)

    def wreg(h, xx, zz, rows):
        return wall.at[h, xx, zz, pl.ds(*rows), :]

    SIGN = (1, -1)

    class Ring:
        def __init__(self, name, h, axis, rows, cut, wide, zz=z):
            self.name, self.h, self.axis = name, h, axis
            self.rows, self.cut, self.wide, self.zz = rows, cut, wide, zz
            self.far = (NX if axis == "x" else NZ) // 2

        def dev(self, d):
            return dp_of(x + SIGN[d], z) if self.axis == "x" else dp_of(x, z + SIGN[d])

        def region(self, d, t):
            rows = self.cut[d] if t == self.far else self.rows
            if self.axis == "x":
                return wreg(self.h, wrap(x - SIGN[d] * t, NX), self.zz, rows)
            return wreg(self.h, ALL if self.wide else x, wrap(z - SIGN[d] * t, NZ), rows)

        def begin(self):
            for d in (0, 1):
                send(self.region(d, 0), W_ID[self.h, self.name, d, 1], self.dev(d))

        def step(self, t):
            for d in (0, 1):
                recv(self.region(d, t), W_ID[self.h, self.name, d, t])
                if t < self.far:
                    hop = self.region(d, t)
                    if t + 1 == self.far:
                        rows = self.cut[d]
                        if self.axis == "x":
                            hop = wreg(self.h, wrap(x - SIGN[d] * t, NX), self.zz, rows)
                        else:
                            hop = wreg(self.h, ALL if self.wide else x, wrap(z - SIGN[d] * t, NZ), rows)
                    send(hop, W_ID[self.h, self.name, d, t + 1], self.dev(d))

    AX = [Ring("ax", h, "x", a_rows, a_half, False) for h in range(HEADS)]
    BZ = [Ring("bz", h, "z", b_rows, bz_half, False) for h in range(HEADS)]
    AZ = [Ring("az", h, "z", a_rows, a_half, True) for h in range(HEADS)]
    BX = [
        {s: Ring(("bx", s), h, "x", b_rows, bx_half, False, wrap(z - s, NZ)) for s in SHIFTS}
        for h in range(HEADS)
    ]

    def begin(h):
        BZ[h].begin()
        AX[h].begin()
        BX[h][0].begin()

    for h in FIRST_HEADS:
        begin(h)

    for n in range(width // BLK):
        gains[:, n * BLK : (n + 1) * BLK] = jnp.broadcast_to(gain[n : n + 1, :].astype(F32), (8, BLK))

    load.wait()
    for t in range(KEEP):
        v = tub[:, t, :].astype(F32)
        v = v - jnp.mean(v, axis=-1, keepdims=True)
        var = jnp.mean(v * v, axis=-1, keepdims=True)
        xn[t * NDP : (t + 1) * NDP, :] = (v * lax.rsqrt(var + 1e-06) * gains[0:1, :]).astype(BF16)

    kept = [keep[e : e + 1, :] >= 0 for e in range(KEEP)]
    mine = [keep[e : e + 1, :] - j_me * KEEP for e in range(KEEP)]
    slots = [slot[e : e + 1, :] for e in range(KEEP)]
    target = []
    for e in range(KEEP):
        rank = jnp.zeros((1, NDP), jnp.int32)
        for f in range(KEEP):
            if f != e:
                rank = rank + jnp.where(kept[f] & (slots[f] < slots[e]), 1, 0)
        target.append(row[e : e + 1, :] * KEEP + rank + 1)
    aims = []
    for t in range(KEEP):
        aim = jnp.zeros((1, NDP), jnp.int32)
        for e in range(KEEP):
            aim = aim + jnp.where(kept[e] & (mine[e] == t), target[e], 0)
        aims.append(aim)
    flat = jnp.concatenate(aims, axis=1) - 1
    r_id = iota((512, BLK), 0)
    hit = ((r_id >> 4) * KEEP + (r_id & 3)) == flat
    pick = jnp.concatenate([one_hot(hit & (((r_id >> 2) & 3) == q)) for q in range(4)], axis=1)
    for n in range(4):
        cols = jnp.concatenate(
            [xn[:, q * 1024 + n * 256 : q * 1024 + (n + 1) * 256] for q in range(4)], axis=0
        )
        moved = jnp.dot(pick, cols, preferred_element_type=F32).astype(BF16)
        snd[:, :, n * 256 : (n + 1) * 256] = moved.reshape(NDP, 16, 256)

    pl.semaphore_wait(entered, len(near))

    def exchange(dx):
        if dx == 0:
            pltpu.make_async_copy(snd.at[p_me], rcv.at[p_me], a2a_r.at[x]).start()

        @pl.loop(1 if dx == 0 else 0, NZ)
        def _(dz):
            dev = dp_of(x + dx, z + dz)
            pltpu.make_async_remote_copy(
                src_ref=snd.at[dev["dp"]], dst_ref=rcv.at[p_me], send_sem=a2a_s,
                recv_sem=a2a_r.at[x], device_id=dev, device_id_type=MESH,
            ).start()

    for dx in FIRST_GROUPS:
        exchange(dx)

    s_id, l_id = iota((BLK, BLK), 0), iota((BLK, BLK), 1)
    lanes = l_id.astype(F32)

    def slot_order():
        for j in range(NT):
            across = seg[:, j * BLK : (j + 1) * BLK].astype(F32)
            down = jnp.sum(jnp.where(s_id == l_id, across, 0.0), axis=1, keepdims=True)
            rank = jnp.sum(jnp.where((down == across) & (l_id < s_id), 1.0, 0.0), axis=1, keepdims=True)
            aim = jnp.where(down >= 0, jnp.floor(down * (1.0 / 32.0)) * KEEP + rank, -1.0)
            hit = jnp.where(aim == lanes, 1.0, 0.0)
            place[j] = hit.astype(BF16)
            present[j : j + 1, :] = jnp.sum(hit, axis=0, keepdims=True)
        wide = iota((BLK, 8 * BLK), 1)
        spread = one_hot(iota((BLK, 8 * BLK), 0) == (wide >> 7) * 16 + (wide & 15))
        valid = jnp.dot(present[...].astype(BF16), spread, preferred_element_type=F32)
        pick_j = ((iota((NT, 8 * BLK), 1) & 127) >> 4) == iota((NT, 8 * BLK), 0)
        valid = jnp.sum(jnp.where(pick_j, valid, 0.0), axis=0, keepdims=True)
        same = ((s_id & 15) >> 2) == ((l_id & 15) >> 2)
        for pg in range(8):
            live = same & (valid[:, pg * BLK : (pg + 1) * BLK] > 0.5)
            bias[pg] = jnp.where(live, 0.0, -1e30)

    o_id, i_id = iota((BLK, BLK), 0), iota((BLK, BLK), 1)
    src = ((o_id & 31) >> 2) * 16 + (o_id >> 5) * 4 + (o_id & 3)
    unpick = one_hot(i_id == src)

    def nreg(j, g, half=None):
        if half is None:
            return nrm.at[j, pl.ds(pl.multiple_of(g * 32, 32), 32), :]
        return nrm.at[j, pl.ds(pl.multiple_of(g * 32 + half * 16, 16), 16), :]

    up, down_, twin = ten_of(y + 1, c), ten_of(y - 1, c), ten_of(y, 1 - c)

    def jdx(yy, cc):
        return wrap(yy, NY) * 2 + cc

    def y_unpack(dx):
        g = wrap(x - dx, NX)
        group = rcv.at[pl.ds(pl.multiple_of(g * NZ, NZ), NZ)]
        pltpu.make_async_copy(group, group, a2a_r.at[g]).wait()
        got = rcv[pl.ds(pl.multiple_of(g * NZ, NZ), NZ)].reshape(BLK, 1024)
        back = jnp.dot(unpick, got, preferred_element_type=F32).astype(BF16)
        at = pl.ds(pl.multiple_of(g * 32, 32), 32)
        for q in range(4):
            nrm[j_me, at, q * 1024 : (q + 1) * 1024] = back[q * 32 : (q + 1) * 32, :]
        own = nreg(j_me, g)
        send(own, Y_ID[dx, "p1"], up)
        send(own, Y_ID[dx, "m1"], down_)
        send(own, Y_ID[dx, "own"], twin)

    def y_near(dx):
        g = wrap(x - dx, NX)
        lo, hi = jdx(y - 1, c), jdx(y + 1, c)
        recv(nreg(lo, g), Y_ID[dx, "p1"])
        send(nreg(lo, g, 0), Y_ID[dx, "p2"], up)
        send(nreg(lo, g), Y_ID[dx, "fp1"], twin)
        recv(nreg(hi, g), Y_ID[dx, "m1"])
        send(nreg(hi, g, 1), Y_ID[dx, "m2"], down_)
        send(nreg(hi, g), Y_ID[dx, "fm1"], twin)

    def y_far(dx):
        g = wrap(x - dx, NX)
        far = jdx(y + 2, c)
        recv(nreg(far, g, 0), Y_ID[dx, "p2"])
        recv(nreg(far, g, 1), Y_ID[dx, "m2"])
        send(nreg(far, g), Y_ID[dx, "f2"], twin)

    def y_twin(dx):
        recv(nreg(jdx(y, 1 - c), wrap(x - dx, NX)), Y_ID[dx, "own"])

    def y_twin_near(dx):
        recv(nreg(jdx(y - 1, 1 - c), wrap(x - dx, NX)), Y_ID[dx, "fp1"])
        recv(nreg(jdx(y + 1, 1 - c), wrap(x - dx, NX)), Y_ID[dx, "fm1"])

    def y_twin_far(dx):
        recv(nreg(jdx(y + 2, 1 - c), wrap(x - dx, NX)), Y_ID[dx, "f2"])

    def weights(name, h, *at):
        if name == "bx":
            BX[h][at[0]].step(at[1])
            return
        t = at[0]
        {"ax": AX, "bz": BZ, "az": AZ}[name][h].step(t)
        if name == "ax" and t == 2:
            AZ[h].begin()
        if name == "bz":
            for s in (t, -t) if t < 4 else (t,):
                BX[h][s].begin()

    def product(h, rows, xx):
        cols = pl.ds(pl.multiple_of(xx * NZ * BLK, BLK), NZ * BLK)
        lhs = nrm[rows, :, cols].reshape(2 * BLK, NZ * BLK)
        rhs = wall[h, xx].reshape(NZ * BLK, 3 * HS)
        return jnp.dot(lhs, rhs, preferred_element_type=F32)

    def qkv_of(h, part, step=0):
        if part == 0:
            rows = pl.ds(2 * wrap(y + (0, 1, -1, 2)[step], NY), 2)
            parts = [product(h, rows, wrap(x + d, NX)) for d in (0, 1, -1)]
            acc[h, rows] = (parts[0] + parts[1] + parts[2]).reshape(2, BLK, 3 * HS)
            return

        for m in range(NT // 2):
            rows = pl.ds(m * 2, 2)
            full = acc[h, rows].reshape(2 * BLK, 3 * HS) + product(h, rows, wrap(x + 2, NX))
            full = full * jnp.where(iota(full.shape, 1) < HS, HS ** (-0.5), 1.0)
            qkv[h, rows] = full.astype(BF16).reshape(2, BLK, 3 * HS)

    def attend(h):
        for pg in range(8):
            part = qkv[h, :, pg * 16 : (pg + 1) * 16, : 2 * HS]
            q, k = part[..., :HS].reshape(BLK, HS), part[..., HS:].reshape(BLK, HS)
            s = lax.dot_general(q, k, (((1,), (1,)), ((), ())), preferred_element_type=F32)
            score[pg] = s + bias[pg]
        for pg in range(8):
            s = score[pg]
            s = jnp.exp(s - jnp.max(s, axis=1, keepdims=True))
            prob[pg] = (s / jnp.sum(s, axis=1, keepdims=True)).astype(BF16)
        for pg in range(8):
            v = qkv[h, :, pg * 16 : (pg + 1) * 16, 2 * HS :].reshape(BLK, HS)
            o = jnp.dot(prob[pg], v, preferred_element_type=F32).astype(BF16)
            att[:, pg * 16 : (pg + 1) * 16, :] = o.reshape(NT, 16, HS)
        for j in range(NT):
            out[j * BLK : (j + 1) * BLK, h * HS : (h + 1) * HS] = jnp.dot(
                place[j], att[j], preferred_element_type=F32
            ).astype(BF16)

    acts = {
        "yu": y_unpack, "yn": y_near, "yf": y_far, "y0": y_twin, "y1": y_twin_near, "y2": y_twin_far, "A": exchange, "W": begin,
        "pl": slot_order, "q": qkv_of, "t": attend,
    }
    for name, *rest in PLAN:
        if name in acts:
            acts[name](*rest)
        else:
            weights(name, *rest)

    for cp in sent:
        cp.wait_send()
    most = snd.at[pl.ds(0, NDP - 1)]
    pltpu.make_async_copy(most, most, a2a_s).wait()


def body(tubelets, keep_index, dest_row, dest_slot, segment, ln_gain, w_query, w_key, w_value):
    width = tubelets.shape[2]
    vmem = pl.BlockSpec(memory_space=pltpu.VMEM)
    hbm = pl.BlockSpec(memory_space=pl.ANY)
    dma = pltpu.SemaphoreType.DMA
    cols = w_query.shape[1]
    mixed = pl.pallas_call(
        kernel,
        out_shape=jax.ShapeDtypeStruct((NT * BLK, cols), BF16),
        in_specs=[hbm] + [vmem] * 5 + [hbm] * 3,
        out_specs=vmem,
        scratch_shapes=[
            pltpu.VMEM(tubelets.shape, BF16),
            pltpu.VMEM((8, width), F32),
            pltpu.VMEM((BLK, width), BF16),
            pltpu.VMEM((NDP, 16, width // 4), BF16),
            pltpu.VMEM((NDP, 16, width // 4), BF16),
            pltpu.VMEM((NT, BLK, width), BF16),
            pltpu.VMEM((HEADS, NX, NZ, BLK, 3 * HS), BF16),
            pltpu.VMEM((HEADS, NT, BLK, 3 * HS), F32),
            pltpu.VMEM((HEADS, NT, BLK, 3 * HS), BF16),
            pltpu.VMEM((NT, BLK, HS), BF16),
            pltpu.VMEM((8, BLK, BLK), F32),
            pltpu.VMEM((8, BLK, BLK), BF16),
            pltpu.VMEM((8, BLK, BLK), F32),
            pltpu.VMEM((NT, BLK, BLK), BF16),
            pltpu.VMEM((NT, BLK), F32),
            dma((3 * HEADS + 1,)),
            dma,
            dma((NX,)),
            dma((N_MSG,)),
            dma((N_MSG,)),
            pltpu.SemaphoreType.REGULAR,
        ],
        compiler_params=pltpu.CompilerParams(
            collective_id=0, has_side_effects=True, vmem_limit_bytes=60 * 1024 * 1024
        ),
        name="repack_attend",
    )(
        tubelets,
        keep_index.T,
        dest_row.T,
        dest_slot.T,
        segment,
        ln_gain.reshape(width // BLK, BLK),
        w_query,
        w_key,
        w_value,
    )
    return mixed.reshape(1, NT * BLK, cols)


def solution(mesh):
    return jax.shard_map(
        body,
        mesh=mesh,
        in_specs=(
            P("dp", "tensor", None),
            P("dp", "tensor"),
            P("dp", "tensor"),
            P("dp", "tensor"),
            P("dp", None),
            P(),
            P("dp", "tensor"),
            P("dp", "tensor"),
            P("dp", "tensor"),
        ),
        out_specs=P("dp", None, "tensor"),
        check_vma=False,
    )
```

```python
import jax
import jax.numpy as jnp
from jax import lax
from jax.experimental import pallas as pl
from jax.experimental.pallas import tpu as pltpu
from jax.sharding import PartitionSpec as P

MESH = pl.DeviceIdType.MESH
F32 = jnp.float32
BF16 = jnp.bfloat16
HS = 128
NX, NZ, NY = 4, 8, 4
NDP, NT = NX * NZ, 2 * NY
KEEP = 4
HEADS = 3
BLK = 128

A_ROWS, A_PLUS = 32, 16
B_ROWS = BLK - A_ROWS
BZ_PLUS, BX_PLUS = 48, 48

SHIFTS = (0, 1, -1, 2, -2, 3, -3, 4)

W_KEYS = (
    [("ax", d, t) for t in (1, 2) for d in (0, 1)]
    + [("bz", d, t) for t in (1, 2, 3, 4) for d in (0, 1)]
    + [("az", d, t) for t in (1, 2, 3, 4) for d in (0, 1)]
    + [(("bx", s), d, t) for s in SHIFTS for t in (1, 2) for d in (0, 1)]
)
W_ID = {(h,) + key: h * len(W_KEYS) + n for h in range(HEADS) for n, key in enumerate(W_KEYS)}
Y_KEYS = ("p1", "m1", "p2", "m2", "own", "fp1", "fm1", "f2")
Y_ID = {(g, key): len(W_ID) + g * len(Y_KEYS) + n for g in range(NX) for n, key in enumerate(Y_KEYS)}
N_MSG = len(W_ID) + len(Y_ID)

PLAN = (
    ("ax", 0, 1), ("bz", 0, 1), ("A", 1), ("bx", 0, 0, 1), ("ax", 1, 1), ("bz", 1, 1), ("bx", 1, 0, 1),
    ("ax", 0, 2), ("bx", 0, 1, 1), ("bx", 0, -1, 1), ("bz", 0, 2), ("A", 3), ("ax", 1, 2), ("yu", 0), ("A", 2),
    ("bx", 1, 1, 1), ("bx", 1, -1, 1), ("bz", 1, 2), ("bx", 0, 2, 1), ("az", 0, 1), ("yn", 0), ("pl",),
    ("bx", 0, -2, 1), ("yu", 1), ("bz", 0, 3), ("yf", 0), ("bx", 1, 2, 1), ("yn", 1), ("yu", 3),
    ("bx", 1, -2, 1), ("bx", 0, 3, 1), ("az", 1, 1), ("yf", 1), ("bx", 0, -3, 1), ("bz", 1, 3), ("yu", 2),
    ("az", 0, 2), ("bz", 0, 4), ("W", 2), ("bx", 1, 3, 1), ("yn", 3), ("bx", 1, -3, 1), ("az", 1, 2),
    ("bz", 1, 4), ("bx", 0, 4, 1), ("ax", 2, 1), ("bx", 2, 0, 1), ("az", 0, 3), ("yn", 2), ("bz", 2, 1),
    ("bx", 1, 4, 1), ("az", 1, 3), ("ax", 2, 2), ("yf", 3), ("az", 0, 4), ("y0", 0), ("y0", 1), ("y0", 3),
    ("y0", 2), ("q", 0, 0, 0), ("y1", 0), ("y1", 1), ("y1", 3), ("y1", 2), ("q", 0, 0, 1), ("bx", 2, 1, 1),
    ("bz", 2, 2), ("yf", 2), ("q", 0, 0, 2), ("bx", 2, -1, 1), ("az", 1, 4), ("q", 1, 0, 0), ("y2", 0),
    ("y2", 1), ("y2", 3), ("y2", 2), ("q", 0, 0, 3), ("az", 2, 1), ("bx", 0, 0, 2), ("bx", 0, 1, 2),
    ("bx", 0, -1, 2), ("bx", 0, 2, 2), ("bx", 0, -2, 2), ("bx", 0, 3, 2), ("bx", 0, -3, 2), ("bx", 0, 4, 2),
    ("q", 0, 1), ("bx", 2, 2, 1), ("bz", 2, 3), ("bx", 2, -2, 1), ("t", 0), ("q", 1, 0, 1), ("az", 2, 2),
    ("q", 1, 0, 2), ("bz", 2, 4), ("q", 1, 0, 3), ("bx", 2, 3, 1), ("bx", 1, 0, 2), ("bx", 1, 1, 2),
    ("bx", 1, -1, 2), ("bx", 1, 2, 2), ("bx", 1, -2, 2), ("bx", 1, 3, 2), ("bx", 1, -3, 2), ("bx", 1, 4, 2),
    ("q", 1, 1), ("bx", 2, -3, 1), ("az", 2, 3), ("t", 1), ("bx", 2, 4, 1), ("az", 2, 4), ("q", 2, 0, 0),
    ("q", 2, 0, 1), ("q", 2, 0, 2), ("q", 2, 0, 3), ("bx", 2, 0, 2), ("bx", 2, 1, 2), ("bx", 2, -1, 2),
    ("bx", 2, 2, 2), ("bx", 2, -2, 2), ("bx", 2, 3, 2), ("bx", 2, -3, 2), ("bx", 2, 4, 2), ("q", 2, 1),
    ("t", 2),
)

FIRST_GROUPS, FIRST_HEADS = (0,), (0, 1)


def iota(shape, dim):
    return lax.broadcasted_iota(jnp.int32, shape, dim)


def one_hot(mask):
    return jnp.where(mask, 1.0, 0.0).astype(BF16)


def kernel(
    tub_hbm, keep, row, slot, seg, gain, wq, wk, wv, out,
    tub, gains, xn, snd, rcv, nrm, wall, acc, qkv, att, score, prob, bias, place, present,
    lsem, a2a_s, a2a_r, ss, rs, entered,
):
    width = xn.shape[1]
    p_me, j_me = lax.axis_index("dp"), lax.axis_index("tensor")
    x, z = p_me // NZ, lax.rem(p_me, NZ)
    y, c = j_me // 2, lax.rem(j_me, 2)

    def wrap(v, n):
        return lax.rem(v + n, n)

    def dp_of(xx, zz):
        return {"dp": wrap(xx, NX) * NZ + wrap(zz, NZ)}

    def ten_of(yy, cc):
        return {"tensor": wrap(yy, NY) * 2 + cc}

    barrier = pltpu.get_barrier_semaphore()
    near = [dp_of(x + d, z) for d in range(1, NX)]
    peers = near + [dp_of(x, z + d) for d in range(1, NZ)]
    peers += [ten_of(y + 1, c), ten_of(y - 1, c), ten_of(y, 1 - c)]
    for dev in peers:
        pl.semaphore_signal(barrier, inc=1, device_id=dev, device_id_type=MESH)

    load = pltpu.make_async_copy(tub_hbm, tub, lsem.at[3 * HEADS])
    load.start()

    local = []
    for h in range(HEADS):
        for n, w in enumerate((wq, wk, wv)):
            cp = pltpu.make_async_copy(
                w.at[:, pl.ds(h * HS, HS)],
                wall.at[h, x, z, :, pl.ds(n * HS, HS)],
                lsem.at[h * 3 + n],
            )
            cp.start()
            local.append(cp)

    pl.semaphore_wait(barrier, len(peers))
    for dev in near:
        pl.semaphore_signal(entered, inc=1, device_id=dev, device_id_type=MESH)
    for cp in local:
        cp.wait()

    sent = []

    def copy(region, n, dev):
        return pltpu.make_async_remote_copy(
            src_ref=region, dst_ref=region, send_sem=ss.at[n], recv_sem=rs.at[n],
            device_id=dev, device_id_type=MESH,
        )

    def send(region, n, dev):
        cp = copy(region, n, dev)
        cp.start()
        sent.append(cp)

    def recv(region, n):
        copy(region, n, dp_of(x + 1, z)).wait_recv()

    ALL = slice(None)
    a_rows, b_rows = (0, A_ROWS), (A_ROWS, B_ROWS)

    def halves(rows, plus):
        return ((rows[0], plus), (rows[0] + plus, rows[1] - plus))

    a_half = halves(a_rows, A_PLUS)
    bz_half, bx_half = halves(b_rows, BZ_PLUS), halves(b_rows, BX_PLUS)

    def wreg(h, xx, zz, rows):
        return wall.at[h, xx, zz, pl.ds(*rows), :]

    SIGN = (1, -1)

    class Ring:
        def __init__(self, name, h, axis, rows, cut, wide, zz=z):
            self.name, self.h, self.axis = name, h, axis
            self.rows, self.cut, self.wide, self.zz = rows, cut, wide, zz
            self.far = (NX if axis == "x" else NZ) // 2

        def dev(self, d):
            return dp_of(x + SIGN[d], z) if self.axis == "x" else dp_of(x, z + SIGN[d])

        def region(self, d, t):
            rows = self.cut[d] if t == self.far else self.rows
            if self.axis == "x":
                return wreg(self.h, wrap(x - SIGN[d] * t, NX), self.zz, rows)
            return wreg(self.h, ALL if self.wide else x, wrap(z - SIGN[d] * t, NZ), rows)

        def begin(self):
            for d in (0, 1):
                send(self.region(d, 0), W_ID[self.h, self.name, d, 1], self.dev(d))

        def step(self, t):
            for d in (0, 1):
                recv(self.region(d, t), W_ID[self.h, self.name, d, t])
                if t < self.far:
                    hop = self.region(d, t)
                    if t + 1 == self.far:
                        rows = self.cut[d]
                        if self.axis == "x":
                            hop = wreg(self.h, wrap(x - SIGN[d] * t, NX), self.zz, rows)
                        else:
                            hop = wreg(self.h, ALL if self.wide else x, wrap(z - SIGN[d] * t, NZ), rows)
                    send(hop, W_ID[self.h, self.name, d, t + 1], self.dev(d))

    AX = [Ring("ax", h, "x", a_rows, a_half, False) for h in range(HEADS)]
    BZ = [Ring("bz", h, "z", b_rows, bz_half, False) for h in range(HEADS)]
    AZ = [Ring("az", h, "z", a_rows, a_half, True) for h in range(HEADS)]
    BX = [
        {s: Ring(("bx", s), h, "x", b_rows, bx_half, False, wrap(z - s, NZ)) for s in SHIFTS}
        for h in range(HEADS)
    ]

    def begin(h):
        BZ[h].begin()
        AX[h].begin()
        BX[h][0].begin()

    for h in FIRST_HEADS:
        begin(h)

    for n in range(width // BLK):
        gains[:, n * BLK : (n + 1) * BLK] = jnp.broadcast_to(gain[n : n + 1, :].astype(F32), (8, BLK))

    load.wait()
    for t in range(KEEP):
        v = tub[:, t, :].astype(F32)
        v = v - jnp.mean(v, axis=-1, keepdims=True)
        var = jnp.mean(v * v, axis=-1, keepdims=True)
        xn[t * NDP : (t + 1) * NDP, :] = (v * lax.rsqrt(var + 1e-06) * gains[0:1, :]).astype(BF16)

    kept = [keep[e : e + 1, :] >= 0 for e in range(KEEP)]
    mine = [keep[e : e + 1, :] - j_me * KEEP for e in range(KEEP)]
    slots = [slot[e : e + 1, :] for e in range(KEEP)]
    target = []
    for e in range(KEEP):
        rank = jnp.zeros((1, NDP), jnp.int32)
        for f in range(KEEP):
            if f != e:
                rank = rank + jnp.where(kept[f] & (slots[f] < slots[e]), 1, 0)
        target.append(row[e : e + 1, :] * KEEP + rank + 1)
    aims = []
    for t in range(KEEP):
        aim = jnp.zeros((1, NDP), jnp.int32)
        for e in range(KEEP):
            aim = aim + jnp.where(kept[e] & (mine[e] == t), target[e], 0)
        aims.append(aim)
    flat = jnp.concatenate(aims, axis=1) - 1
    r_id = iota((512, BLK), 0)
    hit = ((r_id >> 4) * KEEP + (r_id & 3)) == flat
    pick = jnp.concatenate([one_hot(hit & (((r_id >> 2) & 3) == q)) for q in range(4)], axis=1)
    for n in range(4):
        cols = jnp.concatenate(
            [xn[:, q * 1024 + n * 256 : q * 1024 + (n + 1) * 256] for q in range(4)], axis=0
        )
        moved = jnp.dot(pick, cols, preferred_element_type=F32).astype(BF16)
        snd[:, :, n * 256 : (n + 1) * 256] = moved.reshape(NDP, 16, 256)

    pl.semaphore_wait(entered, len(near))

    def exchange(dx):
        if dx == 0:
            pltpu.make_async_copy(snd.at[p_me], rcv.at[p_me], a2a_r.at[x]).start()

        @pl.loop(1 if dx == 0 else 0, NZ)
        def _(dz):
            dev = dp_of(x + dx, z + dz)
            pltpu.make_async_remote_copy(
                src_ref=snd.at[dev["dp"]], dst_ref=rcv.at[p_me], send_sem=a2a_s,
                recv_sem=a2a_r.at[x], device_id=dev, device_id_type=MESH,
            ).start()

    for dx in FIRST_GROUPS:
        exchange(dx)

    s_id, l_id = iota((BLK, BLK), 0), iota((BLK, BLK), 1)
    lanes = l_id.astype(F32)

    def slot_order():
        for j in range(NT):
            across = seg[:, j * BLK : (j + 1) * BLK].astype(F32)
            down = jnp.sum(jnp.where(s_id == l_id, across, 0.0), axis=1, keepdims=True)
            rank = jnp.sum(jnp.where((down == across) & (l_id < s_id), 1.0, 0.0), axis=1, keepdims=True)
            aim = jnp.where(down >= 0, jnp.floor(down * (1.0 / 32.0)) * KEEP + rank, -1.0)
            hit = jnp.where(aim == lanes, 1.0, 0.0)
            place[j] = hit.astype(BF16)
            present[j : j + 1, :] = jnp.sum(hit, axis=0, keepdims=True)
        wide = iota((BLK, 8 * BLK), 1)
        spread = one_hot(iota((BLK, 8 * BLK), 0) == (wide >> 7) * 16 + (wide & 15))
        valid = jnp.dot(present[...].astype(BF16), spread, preferred_element_type=F32)
        pick_j = ((iota((NT, 8 * BLK), 1) & 127) >> 4) == iota((NT, 8 * BLK), 0)
        valid = jnp.sum(jnp.where(pick_j, valid, 0.0), axis=0, keepdims=True)
        same = ((s_id & 15) >> 2) == ((l_id & 15) >> 2)
        for pg in range(8):
            live = same & (valid[:, pg * BLK : (pg + 1) * BLK] > 0.5)
            bias[pg] = jnp.where(live, 0.0, -1e30)

    o_id, i_id = iota((BLK, BLK), 0), iota((BLK, BLK), 1)
    src = ((o_id & 31) >> 2) * 16 + (o_id >> 5) * 4 + (o_id & 3)
    unpick = one_hot(i_id == src)

    def nreg(j, g, half=None):
        if half is None:
            return nrm.at[j, pl.ds(pl.multiple_of(g * 32, 32), 32), :]
        return nrm.at[j, pl.ds(pl.multiple_of(g * 32 + half * 16, 16), 16), :]

    up, down_, twin = ten_of(y + 1, c), ten_of(y - 1, c), ten_of(y, 1 - c)

    def jdx(yy, cc):
        return wrap(yy, NY) * 2 + cc

    def y_unpack(dx):
        g = wrap(x - dx, NX)
        group = rcv.at[pl.ds(pl.multiple_of(g * NZ, NZ), NZ)]
        pltpu.make_async_copy(group, group, a2a_r.at[g]).wait()
        got = rcv[pl.ds(pl.multiple_of(g * NZ, NZ), NZ)].reshape(BLK, 1024)
        back = jnp.dot(unpick, got, preferred_element_type=F32).astype(BF16)
        at = pl.ds(pl.multiple_of(g * 32, 32), 32)
        for q in range(4):
            nrm[j_me, at, q * 1024 : (q + 1) * 1024] = back[q * 32 : (q + 1) * 32, :]
        own = nreg(j_me, g)
        send(own, Y_ID[dx, "p1"], up)
        send(own, Y_ID[dx, "m1"], down_)
        send(own, Y_ID[dx, "own"], twin)

    def y_near(dx):
        g = wrap(x - dx, NX)
        lo, hi = jdx(y - 1, c), jdx(y + 1, c)
        recv(nreg(lo, g), Y_ID[dx, "p1"])
        send(nreg(lo, g, 0), Y_ID[dx, "p2"], up)
        send(nreg(lo, g), Y_ID[dx, "fp1"], twin)
        recv(nreg(hi, g), Y_ID[dx, "m1"])
        send(nreg(hi, g, 1), Y_ID[dx, "m2"], down_)
        send(nreg(hi, g), Y_ID[dx, "fm1"], twin)

    def y_far(dx):
        g = wrap(x - dx, NX)
        far = jdx(y + 2, c)
        recv(nreg(far, g, 0), Y_ID[dx, "p2"])
        recv(nreg(far, g, 1), Y_ID[dx, "m2"])
        send(nreg(far, g), Y_ID[dx, "f2"], twin)

    def y_twin(dx):
        recv(nreg(jdx(y, 1 - c), wrap(x - dx, NX)), Y_ID[dx, "own"])

    def y_twin_near(dx):
        recv(nreg(jdx(y - 1, 1 - c), wrap(x - dx, NX)), Y_ID[dx, "fp1"])
        recv(nreg(jdx(y + 1, 1 - c), wrap(x - dx, NX)), Y_ID[dx, "fm1"])

    def y_twin_far(dx):
        recv(nreg(jdx(y + 2, 1 - c), wrap(x - dx, NX)), Y_ID[dx, "f2"])

    def weights(name, h, *at):
        if name == "bx":
            BX[h][at[0]].step(at[1])
            return
        t = at[0]
        {"ax": AX, "bz": BZ, "az": AZ}[name][h].step(t)
        if name == "ax" and t == 2:
            AZ[h].begin()
        if name == "bz":
            for s in (t, -t) if t < 4 else (t,):
                BX[h][s].begin()

    def product(h, rows, xx):
        cols = pl.ds(pl.multiple_of(xx * NZ * BLK, BLK), NZ * BLK)
        lhs = nrm[rows, :, cols].reshape(2 * BLK, NZ * BLK)
        rhs = wall[h, xx].reshape(NZ * BLK, 3 * HS)
        return jnp.dot(lhs, rhs, preferred_element_type=F32)

    def qkv_of(h, part, step=0):
        if part == 0:
            rows = pl.ds(2 * wrap(y + (0, 1, -1, 2)[step], NY), 2)
            parts = [product(h, rows, wrap(x + d, NX)) for d in (0, 1, -1)]
            acc[h, rows] = (parts[0] + parts[1] + parts[2]).reshape(2, BLK, 3 * HS)
            return

        for m in range(NT // 2):
            rows = pl.ds(m * 2, 2)
            full = acc[h, rows].reshape(2 * BLK, 3 * HS) + product(h, rows, wrap(x + 2, NX))
            full = full * jnp.where(iota(full.shape, 1) < HS, HS ** (-0.5), 1.0)
            qkv[h, rows] = full.astype(BF16).reshape(2, BLK, 3 * HS)

    def attend(h):
        for pg in range(8):
            part = qkv[h, :, pg * 16 : (pg + 1) * 16, : 2 * HS]
            q, k = part[..., :HS].reshape(BLK, HS), part[..., HS:].reshape(BLK, HS)
            s = lax.dot_general(q, k, (((1,), (1,)), ((), ())), preferred_element_type=F32)
            score[pg] = s + bias[pg]
        for pg in range(8):
            s = score[pg]
            s = jnp.exp(s - jnp.max(s, axis=1, keepdims=True))
            prob[pg] = (s / jnp.sum(s, axis=1, keepdims=True)).astype(BF16)
        for pg in range(8):
            v = qkv[h, :, pg * 16 : (pg + 1) * 16, 2 * HS :].reshape(BLK, HS)
            o = jnp.dot(prob[pg], v, preferred_element_type=F32).astype(BF16)
            att[:, pg * 16 : (pg + 1) * 16, :] = o.reshape(NT, 16, HS)
        for j in range(NT):
            out[j * BLK : (j + 1) * BLK, h * HS : (h + 1) * HS] = jnp.dot(
                place[j], att[j], preferred_element_type=F32
            ).astype(BF16)

    acts = {
        "yu": y_unpack, "yn": y_near, "yf": y_far, "y0": y_twin, "y1": y_twin_near, "y2": y_twin_far, "A": exchange, "W": begin,
        "pl": slot_order, "q": qkv_of, "t": attend,
    }
    for name, *rest in PLAN:
        if name in acts:
            acts[name](*rest)
        else:
            weights(name, *rest)

    for cp in sent:
        cp.wait_send()
    most = snd.at[pl.ds(0, NDP - 1)]
    pltpu.make_async_copy(most, most, a2a_s).wait()


def body(tubelets, keep_index, dest_row, dest_slot, segment, ln_gain, w_query, w_key, w_value):
    width = tubelets.shape[2]
    vmem = pl.BlockSpec(memory_space=pltpu.VMEM)
    hbm = pl.BlockSpec(memory_space=pl.ANY)
    dma = pltpu.SemaphoreType.DMA
    cols = w_query.shape[1]
    mixed = pl.pallas_call(
        kernel,
        out_shape=jax.ShapeDtypeStruct((NT * BLK, cols), BF16),
        in_specs=[hbm] + [vmem] * 5 + [hbm] * 3,
        out_specs=vmem,
        scratch_shapes=[
            pltpu.VMEM(tubelets.shape, BF16),
            pltpu.VMEM((8, width), F32),
            pltpu.VMEM((BLK, width), BF16),
            pltpu.VMEM((NDP, 16, width // 4), BF16),
            pltpu.VMEM((NDP, 16, width // 4), BF16),
            pltpu.VMEM((NT, BLK, width), BF16),
            pltpu.VMEM((HEADS, NX, NZ, BLK, 3 * HS), BF16),
            pltpu.VMEM((HEADS, NT, BLK, 3 * HS), F32),
            pltpu.VMEM((HEADS, NT, BLK, 3 * HS), BF16),
            pltpu.VMEM((NT, BLK, HS), BF16),
            pltpu.VMEM((8, BLK, BLK), F32),
            pltpu.VMEM((8, BLK, BLK), BF16),
            pltpu.VMEM((8, BLK, BLK), F32),
            pltpu.VMEM((NT, BLK, BLK), BF16),
            pltpu.VMEM((NT, BLK), F32),
            dma((3 * HEADS + 1,)),
            dma,
            dma((NX,)),
            dma((N_MSG,)),
            dma((N_MSG,)),
            pltpu.SemaphoreType.REGULAR,
        ],
        compiler_params=pltpu.CompilerParams(
            collective_id=0, has_side_effects=True, vmem_limit_bytes=60 * 1024 * 1024
        ),
        name="repack_attend",
    )(
        tubelets,
        keep_index.T,
        dest_row.T,
        dest_slot.T,
        segment,
        ln_gain.reshape(width // BLK, BLK),
        w_query,
        w_key,
        w_value,
    )
    return mixed.reshape(1, NT * BLK, cols)


def solution(mesh):
    return jax.shard_map(
        body,
        mesh=mesh,
        in_specs=(
            P("dp", "tensor", None),
            P("dp", "tensor"),
            P("dp", "tensor"),
            P("dp", "tensor"),
            P("dp", None),
            P(),
            P("dp", "tensor"),
            P("dp", "tensor"),
            P("dp", "tensor"),
        ),
        out_specs=P("dp", None, "tensor"),
        check_vma=False,
    )
```
